32 devices in a mesh: tile: 16 (over z, y, x), lev: 2 (over core).
Axes of the slice: x: 2, y: 2, z: 4, core: 2. Of those that a mesh axis runs over, the one named last changes fastest.
Arguments:
- fields: float32 [2, 32, 81920], P(None, 'lev', 'tile'), may hold values from -6 to 6
- neighbors: int32 [3, 81920], P(None, 'tile'), may hold values from 0 to 5375, as said below
- diffusion: float32 [3, 81920], P(None, 'tile'), may hold values from 0.03 to 0.3
- ancillary: bfloat16 [493, 81920], P(None, 'tile'), may hold values from -6 to 6
- convecting_groups_per_patch: int32 [16, 32], P('tile'), may hold values from 0 to 39, as said below
- owners: int32 [16, 32], P('tile'), may hold values from 0 to 7, as said below
- first_weight: bfloat16 [16, 557, 256], P('tile'), may hold values from -0.25 to 0.25
- first_bias: bfloat16 [16, 256], P('tile'), may hold values from -3 to 3
- middle_weight: bfloat16 [16, 2, 512, 256], P('tile'), may hold values from -0.25 to 0.25
- middle_bias: bfloat16 [16, 2, 256], P('tile'), may hold values from -3 to 3
- last_weight: bfloat16 [16, 256, 64], P('tile'), may hold values from -0.25 to 0.25
- last_bias: bfloat16 [16, 32], P('tile'), may hold values from -3 to 3
Outputs:
- updated: float32 [2, 32, 81920], P(None, 'lev', 'tile')
The draws below stay inside these ranges and needn't reach their ends.
Inputs may be any that keep to these rules, and one draw needn't show every extreme that they name: `neighbors`: A tile's extended row has 5376 positions; the neighbours of the cell at position i of its tile lie at extended positions within 128 of 128 + i. `convecting_groups_per_patch`: the blocks listed in one tile's row are distinct. `owners`: in each half of a tile's row (slots 0 to 15 and the rest) no network is named more than twice; one network, the same in every row, is named exactly twice in every half.
All inputs are finite; a program needn't handle non-finite values.
Results may differ from the reference program's by a relative error of at most 0.0035.
Values may be sent and summed in bfloat16 or wider, within the bound.
No kernel may reach another device: no remote copies, remote signals or barrier semaphores. Data moves between devices by JAX's collectives and lax.ppermute only.
A program may use at most 128 MiB of HBM per device.

```python
import math
import jax
import jax.numpy as jnp
from jax import lax

LEVELS = 32
FEATURES = 557
HIDDEN_SIZE = 512
MID_LAYERS = 2
BLOCK_COLS = 128
BLOCKS = 40
ACTIVE = 32
RIM_CELLS = 128
SUBSTEPS = 5
CELLS_TILE = 5120
CELLS = 81920
ANCILLARY = 493
OUTPUTS = 64
NETWORKS = 8
N_TILE = 16


def draw_neighbors(key, part):
    offsets = jax.random.randint(jax.random.fold_in(key, 1), (3, CELLS), 1, RIM_CELLS + 1)
    direction = jax.random.randint(jax.random.fold_in(key, 2), (3, CELLS), 0, 2) * 2 - 1
    position = jnp.arange(CELLS, dtype=jnp.int32) % CELLS_TILE
    moved = offsets * direction
    first_edge = jnp.arange(3)[:, None] == 0
    moved = jnp.where(first_edge & (position == 0)[None, :], -RIM_CELLS, moved)
    moved = jnp.where(first_edge & (position == CELLS_TILE - 1)[None, :], RIM_CELLS, moved)
    return (RIM_CELLS + position[None, :] + moved).astype(jnp.int32)


def draw_convecting_groups_per_patch(key, part):
    row_keys = jax.random.split(jax.random.fold_in(key, 5), 2 * NETWORKS)
    picked = jax.vmap(lambda row_key: jax.random.permutation(row_key, BLOCKS)[:ACTIVE])(row_keys)
    return picked.astype(jnp.int32)


def draw_owners(key, part):
    half_count = ACTIVE // 2
    busiest = jax.random.randint(jax.random.fold_in(key, 7), (), 0, NETWORKS).astype(jnp.int32)
    candidates = (jnp.arange(2 * NETWORKS, dtype=jnp.int32) // 2).astype(jnp.int32)

    def one_row(row_key):
        shuffled = jax.random.permutation(jax.random.fold_in(row_key, 1), 2 * NETWORKS).astype(jnp.int32)
        priority = shuffled + (candidates == busiest).astype(jnp.int32) * (4 * NETWORKS)
        others = candidates[jnp.argsort(priority)][:half_count - 2]
        picked = jnp.concatenate([jnp.stack([busiest, busiest]), others])
        placement = jax.random.permutation(jax.random.fold_in(row_key, 2), half_count)
        return picked[placement]
    row_keys = jax.random.split(jax.random.fold_in(key, 3), 4 * NETWORKS)
    return jax.vmap(one_row)(row_keys).reshape(2 * NETWORKS, ACTIVE).astype(jnp.int32)


def levels(stream_key, shape, cuts, smallest, largest):
    def one(axis_at, blocks):
        draws = jax.random.uniform(jax.random.fold_in(jax.random.fold_in(stream_key, 6), axis_at), (blocks,), jnp.float32, smallest / len(cuts), largest / len(cuts))
        return jnp.repeat(jnp.exp(draws), shape[axis_at] // blocks).reshape((-1,) + (1,) * (len(shape) - axis_at - 1))

    loudness = one(*cuts[0])
    for cut in cuts[1:]:
        loudness = loudness * one(*cut)
    return loudness


def normal_values(key, dims, spread, most, pieces=(), held_as=jnp.bfloat16):
    gain = levels(key, dims, pieces, -0.22, 0.18) if pieces else 1.0
    result = jax.random.normal(key, dims, jnp.float32) * spread * gain
    return jnp.minimum(jnp.maximum(result, -most), most).astype(held_as)


def setup_inputs(seed: int = 0) -> dict:
    key_of = jax.random.split(jax.random.key(seed), 13)
    fields = normal_values(key_of[0], (2, LEVELS, CELLS), 1.0, 6.0, ((1, 2), (2, 16)), jnp.float32)
    neighbors = draw_neighbors(jax.random.fold_in(key_of[12], 71), 0)
    diffusion = jnp.clip(jnp.exp(math.log(0.3) - 2.3025852 * jax.random.uniform(key_of[2], (3, CELLS), jnp.float32) ** levels(key_of[2], (3, CELLS), ((1, 16),), -0.2, 0.2)), 0.03, 0.3)
    ancillary = normal_values(key_of[3], (ANCILLARY, CELLS), 1.0, 6.0, ((1, 16),))
    convecting_groups_per_patch = draw_convecting_groups_per_patch(jax.random.fold_in(key_of[12], 71), 0)
    owners = draw_owners(jax.random.fold_in(key_of[12], 71), 0)
    first_weight = normal_values(key_of[6], (2 * NETWORKS, FEATURES, HIDDEN_SIZE // 2), FEATURES ** -0.5, 0.25, ((0, 16),))
    first_bias = normal_values(key_of[7], (2 * NETWORKS, HIDDEN_SIZE // 2), 0.5, 3.0, ((0, 16),))
    middle_weight = normal_values(key_of[8], (2 * NETWORKS, MID_LAYERS, HIDDEN_SIZE, HIDDEN_SIZE // 2), HIDDEN_SIZE ** -0.5, 0.25, ((0, 16),))
    middle_bias = normal_values(key_of[9], (2 * NETWORKS, MID_LAYERS, HIDDEN_SIZE // 2), 0.5, 3.0, ((0, 16),))
    last_weight = normal_values(key_of[10], (2 * NETWORKS, HIDDEN_SIZE // 2, OUTPUTS), HIDDEN_SIZE ** -0.5, 0.25, ((0, 16),))
    last_bias = normal_values(key_of[11], (2 * NETWORKS, OUTPUTS // 2), 0.5, 3.0, ((0, 16),))
    return {"fields": fields, "neighbors": neighbors, "diffusion": diffusion, "ancillary": ancillary, "convecting_groups_per_patch": convecting_groups_per_patch, "owners": owners, "first_weight": first_weight, "first_bias": first_bias, "middle_weight": middle_weight, "middle_bias": middle_bias, "last_weight": last_weight, "last_bias": last_bias}


coupling = 0.25


def spread_term(tiled, extended, neighbor_rows, diffusion_rows):
    running = jnp.zeros_like(tiled)
    for side_index in range(3):
        chosen = jnp.broadcast_to(neighbor_rows[side_index], tiled.shape)
        beside = jnp.take_along_axis(extended, chosen, axis=3)
        running = running + diffusion_rows[side_index] * (beside - tiled)
    return running


def affine(activation_values, weight_matrix, shift):
    return jnp.dot(weight_matrix.T, activation_values, preferred_element_type=jnp.float32) + shift.astype(jnp.float32)[:, None]


def reference(fields, neighbors, diffusion, ancillary, convecting_groups_per_patch, owners, first_weight, first_bias, middle_weight, middle_bias, last_weight, last_bias):
    half_hidden = HIDDEN_SIZE // 2
    tiled = fields.reshape(2, LEVELS, N_TILE, CELLS_TILE)
    neighbor_rows = neighbors.reshape(3, N_TILE, CELLS_TILE)
    diffusion_rows = diffusion.reshape(3, N_TILE, CELLS_TILE)
    current = tiled
    for substep in range(SUBSTEPS):
        before = jnp.roll(current, 1, axis=2)[..., CELLS_TILE - RIM_CELLS:]
        after = jnp.roll(current, -1, axis=2)[..., :RIM_CELLS]
        extended = jnp.concatenate([before, current, after], axis=3)
        padded_rows = jnp.pad(current, ((0, 0), (1, 1), (0, 0), (0, 0)))
        vertical = padded_rows[:, 2:] - padded_rows[:, :-2]
        current = current + spread_term(current, extended, neighbor_rows, diffusion_rows) - coupling * vertical[::-1]
    column_state = tiled.astype(jnp.bfloat16).reshape(2, LEVELS, N_TILE, BLOCKS, BLOCK_COLS)
    ground_quantity = ancillary.reshape(ANCILLARY, N_TILE, BLOCKS, BLOCK_COLS)
    first_full = first_weight.reshape(NETWORKS, 2, FEATURES, half_hidden).transpose(0, 2, 1, 3).reshape(NETWORKS, FEATURES, HIDDEN_SIZE)
    first_shift = first_bias.reshape(NETWORKS, HIDDEN_SIZE)
    middle_full = middle_weight.reshape(NETWORKS, 2, MID_LAYERS, HIDDEN_SIZE, half_hidden).transpose(0, 2, 3, 1, 4).reshape(NETWORKS, MID_LAYERS, HIDDEN_SIZE, HIDDEN_SIZE)
    middle_shift = middle_bias.reshape(NETWORKS, 2, MID_LAYERS, half_hidden).transpose(0, 2, 1, 3).reshape(NETWORKS, MID_LAYERS, HIDDEN_SIZE)
    last_full = last_weight.reshape(NETWORKS, HIDDEN_SIZE, OUTPUTS)
    last_shift = last_bias.reshape(NETWORKS, OUTPUTS)
    tile_ids = jnp.broadcast_to(jnp.arange(N_TILE, dtype=jnp.int32)[:, None], (N_TILE, ACTIVE))

    def evaluate(slot_entry):
        tile_id, block_id, owner_id = slot_entry
        column = column_state[:, :, tile_id, block_id, :].reshape(2 * LEVELS, BLOCK_COLS)
        inputs = jnp.concatenate([column, ground_quantity[:, tile_id, block_id, :]], axis=0)
        hidden = jax.nn.silu(affine(inputs, first_full[owner_id], first_shift[owner_id])).astype(jnp.bfloat16)
        for layer_index in range(MID_LAYERS):
            hidden = jax.nn.silu(affine(hidden, middle_full[owner_id, layer_index], middle_shift[owner_id, layer_index])).astype(jnp.bfloat16)
        return affine(hidden, last_full[owner_id], last_shift[owner_id]).astype(jnp.bfloat16)

    evaluated = lax.map(evaluate, (tile_ids.reshape(-1), convecting_groups_per_patch.reshape(-1).astype(jnp.int32), owners.reshape(-1).astype(jnp.int32)))
    placed = evaluated.reshape(N_TILE, ACTIVE, 2, LEVELS, BLOCK_COLS).transpose(2, 3, 0, 1, 4).astype(jnp.float32)
    tendency = jnp.zeros((2, LEVELS, N_TILE, BLOCKS, BLOCK_COLS), jnp.float32)
    tendency = tendency.at[:, :, tile_ids, convecting_groups_per_patch, :].set(placed)
    return current.reshape(2, LEVELS, CELLS) + tendency.reshape(2, LEVELS, CELLS)
```

```python
import functools
import jax
import jax.numpy as jnp
from jax import lax
from jax.experimental import pallas as pl
from jax.experimental.pallas import tpu as pltpu
from jax.sharding import PartitionSpec as P

COLS = 128
STEPS = 5
COUPLING = 0.25
PAD = 8
BF16 = jnp.bfloat16
F32 = jnp.float32


VM = pl.BlockSpec(memory_space=pltpu.VMEM)
SM = pl.BlockSpec(memory_space=pltpu.SMEM)
ANY = pl.BlockSpec(memory_space=pl.ANY)


def ceil16(count):
    return -(-count // 16) * 16


def block(b):
    return pl.ds(pl.multiple_of(b * COLS, COLS), COLS)


def lanes(values, index):
    return jnp.take_along_axis(values, index, axis=1, mode="promise_in_bounds")


def weight_rows(first, middle, last):
    inputs = ceil16(first.shape[0])
    hidden = middle.shape[0] * middle.shape[1]
    return inputs, inputs + hidden, inputs + hidden + last.shape[1]


def join_kernel(state, first, first_bias, middle, middle_bias, last, last_bias, out, part):
    tile = lax.axis_index("tile")
    lev = lax.axis_index("lev")
    surface = first.shape[0] - state
    inputs, tail, bias = weight_rows(first, middle, last)
    width = first.shape[1]
    out[inputs - state - 16 : inputs - state] = jnp.zeros((16, width), BF16)
    out[0:surface] = first[state:]
    out[inputs - state : inputs] = first[0:state]
    depth = middle.shape[1]
    for i in range(middle.shape[0]):
        out[inputs + i * depth : inputs + (i + 1) * depth] = middle[i]
    out[tail:bias] = last[...].astype(F32).T.astype(BF16)
    ends = last_bias[...].astype(F32)
    blank = jnp.zeros((1, ends.shape[1]), F32)
    low = tile % 2 == 0
    row = jnp.concatenate([jnp.where(low, ends, blank), jnp.where(low, blank, ends)], axis=1)
    rows = [first_bias[...].astype(F32)]
    rows += [middle_bias[i : i + 1].astype(F32) for i in range(middle.shape[0])]
    rows += [jnp.pad(row, ((0, 0), (0, width - row.shape[1])))]
    rows += [jnp.zeros((16 - len(rows), width), F32)]
    out[bias:] = jnp.concatenate(rows, axis=0).astype(BF16)
    half = part.shape[0]
    part[...] = out[pl.ds(pl.multiple_of(lev * half, 16), half)]


def joined_weights(state, first, first_bias, middle, middle_bias, last, last_bias):
    rows = weight_rows(first, middle, last)[2] + 16
    return pl.pallas_call(
        functools.partial(join_kernel, state),
        out_shape=(
            jax.ShapeDtypeStruct((rows, first.shape[1]), BF16),
            jax.ShapeDtypeStruct((rows // 2, first.shape[1]), BF16),
        ),
        in_specs=[VM] * 6,
        out_specs=(VM, VM),
        name="join_weights",
    )(first, first_bias, middle, middle_bias, last, last_bias)


def fill_slots(listed, owners, half, table, row, seen, empty):
    tile = lax.axis_index("tile")
    positions = lax.axis_size("tile") // 4
    high = tile // (2 * positions)
    place = (tile % (2 * positions)) // 2
    count = listed.shape[1] // 2

    def wipe(i, carry):
        table[row, i] = empty
        return carry

    lax.fori_loop(0, 4 * positions, wipe, 0)

    def unsee(i, carry):
        seen[i] = 0
        return carry

    lax.fori_loop(0, 2 * positions, unsee, 0)

    def put(s, carry):
        at = half * count + s
        owner = owners[0, at]
        rank = seen[owner]
        seen[owner] = rank + 1
        chunk = (owner % positions) ^ place
        sub = (owner // positions) ^ high
        table[row, chunk * 4 + sub * 2 + rank] = listed[0, at]
        return carry

    lax.fori_loop(0, count, put, 0)


def dispatch_kernel(listed, owners, fields, other, near, spread, surface, *refs):
    positions = lax.axis_size("tile") // 4
    chunks = refs[:positions]
    to_next, to_last, stage, packed, table, seen, sems, out_sems = refs[positions:]
    lev = lax.axis_index("lev")
    slots = 4 * positions
    blocks = fields.shape[2] // COLS
    deep = fields.shape[1]
    base = packed.shape[1] - 4 * deep
    fill_slots(listed, owners, lev, table, 0, seen, 0)

    def copy(slot):
        return pltpu.make_async_copy(
            surface.at[:, block(table[0, slot])], stage.at[slot], sems.at[slot]
        )

    def start(slot, carry):
        copy(slot).start()
        return carry

    lax.fori_loop(0, slots, start, 0)

    def states(slot, carry):
        cols = block(table[0, slot])
        packed[slot, base - 16 : base] = jnp.zeros((16, COLS), BF16)
        for f in range(2):
            mine = pl.multiple_of(base + 2 * deep * f + deep * lev, 16)
            theirs = pl.multiple_of(base + 2 * deep * f + deep * (1 - lev), 16)
            packed[slot, pl.ds(mine, deep)] = fields[f, :, cols].astype(BF16)
            packed[slot, pl.ds(theirs, deep)] = other[f, :, cols].astype(BF16)
        return carry

    lax.fori_loop(0, slots, states, 0)
    outs = [
        pltpu.make_async_copy(packed.at[4 * m : 4 * m + 4], chunks[m], out_sems.at[m])
        for m in range(positions)
    ]
    for m in list(range(1, positions)) + [0]:

        def finish(i, carry, m=m):
            slot = 4 * m + i
            copy(slot).wait()
            packed[slot, 0 : stage.shape[1]] = stage[slot]
            return carry

        lax.fori_loop(0, 4, finish, 0)
        outs[m].start()

    near_lev = pl.multiple_of(8 * lev, 8)
    here = pl.multiple_of(8 * lev, 8)
    there = pl.multiple_of(deep * (1 - lev), 8)
    window = deep + 8
    for rim, begin in ((to_next, blocks - STEPS), (to_last, 0)):
        for b in range(STEPS):
            cols = slice((begin + b) * COLS, (begin + b + 1) * COLS)
            for f in range(2):
                rim[b, pl.ds(f * window + here, deep)] = fields[f, :, cols]
                rim[b, pl.ds(f * window + there, 8)] = other[f, pl.ds(near_lev, 8), cols]
            tail = [
                (near[:, cols] - (begin + b) * COLS).astype(F32),
                spread[:, cols],
                jnp.zeros((2, COLS), F32),
            ]
            rim[b, 2 * window :] = jnp.concatenate(tail, axis=0)
    for out in outs:
        out.wait()


def dispatched(listed, owners, fields, other, near, spread, surface):
    positions = lax.axis_size("tile") // 4
    slots = 4 * positions
    deep = fields.shape[1]
    rows = ceil16(surface.shape[0]) + 4 * deep
    rim = jax.ShapeDtypeStruct((STEPS, 2 * (deep + 8) + 8, COLS), F32)
    return pl.pallas_call(
        dispatch_kernel,
        out_shape=[jax.ShapeDtypeStruct((4, rows, COLS), BF16)] * positions + [rim, rim],
        in_specs=[SM, SM, VM, VM, VM, VM, ANY],
        out_specs=[ANY] * positions + [VM, VM],
        scratch_shapes=[
            pltpu.VMEM((slots, surface.shape[0], COLS), BF16),
            pltpu.VMEM((slots, rows, COLS), BF16),
            pltpu.SMEM((1, slots), jnp.int32),
            pltpu.SMEM((2 * positions,), jnp.int32),
            pltpu.SemaphoreType.DMA((slots,)),
            pltpu.SemaphoreType.DMA((positions,)),
        ],
        name="dispatch",
    )(listed, owners, fields, other, near, spread, surface)


def dynamics_kernel(fields, other, near, spread, left, right, out, first, second, where, coef):
    lev = lax.axis_index("lev")
    deep = fields.shape[1]
    window = deep + 8
    blocks = fields.shape[2] // COLS
    total = blocks + 2 * STEPS
    own_row = pl.multiple_of(PAD + 8 * lev, 8)
    far_row = pl.multiple_of(PAD + deep * (1 - lev), 8)
    far_from = pl.multiple_of(8 * lev, 8)
    zeros = jnp.zeros((PAD, COLS), F32)

    def clear(b, carry):
        for buf in (first, second):
            for f in range(2):
                buf[b, f, 0:PAD] = zeros
                buf[b, f, PAD + window :] = zeros
        return carry

    lax.fori_loop(0, total, clear, 0)

    def fill(b, carry):
        cols = block(b)
        for f in range(2):
            first[b + STEPS, f, pl.ds(own_row, deep)] = fields[f, :, cols]
            first[b + STEPS, f, pl.ds(far_row, 8)] = other[f, pl.ds(far_from, 8), cols]
        where[b + STEPS, 0:3] = near[:, cols] - b * COLS
        coef[b + STEPS, 0:3] = spread[:, cols]
        return carry

    lax.fori_loop(0, blocks, fill, 0)
    for base, rim in ((0, left), (STEPS + blocks, right)):
        for b in range(STEPS):
            for f in range(2):
                first[base + b, f, PAD : PAD + window] = rim[b, f * window : (f + 1) * window]
            where[base + b, 0:3] = rim[b, 2 * window : 2 * window + 3].astype(jnp.int32)
            coef[base + b, 0:3] = rim[b, 2 * window + 3 : 2 * window + 6]

    groups = [(f, v) for f in range(2) for v in range(window // 8)]
    for step in range(STEPS):
        src, dst = (first, second) if step % 2 == 0 else (second, first)

        def advance(b, carry, src=src, dst=dst):
            here = {}
            acc = {}
            for f, v in groups:
                low = PAD + 8 * v
                here[f, v] = src[b, f, low : low + 8]
                above = src[b, 1 - f, low + 1 : low + 9]
                below = src[b, 1 - f, low - 1 : low + 7]
                acc[f, v] = here[f, v] - COUPLING * (above - below)
            for k in range(3):
                pos = jnp.broadcast_to(where[b, k : k + 1], (8, COLS))
                pick = pos & (COLS - 1)
                side = pos // COLS
                weight = jnp.broadcast_to(coef[b, k : k + 1], (8, COLS))
                for f, v in groups:
                    rows = slice(PAD + 8 * v, PAD + 8 * v + 8)
                    own = lanes(here[f, v], pick)
                    before = lanes(src[b - 1, f, rows], pick)
                    after = lanes(src[b + 1, f, rows], pick)
                    beside = jnp.where(side == 1, own, jnp.where(side == 0, before, after))
                    acc[f, v] = acc[f, v] + weight * (beside - here[f, v])
            for f, v in groups:
                dst[b, f, PAD + 8 * v : PAD + 8 * v + 8] = acc[f, v]
            return carry

        lax.fori_loop(step + 1, total - 1 - step, advance, 0, unroll=2)
    last = second if STEPS % 2 == 1 else first

    def emit(b, carry):
        for f in range(2):
            out[f, :, block(b)] = last[b + STEPS, f, pl.ds(own_row, deep)]
        return carry

    lax.fori_loop(0, blocks, emit, 0)


def dynamics(fields, other, near, spread, left, right):
    total = fields.shape[2] // COLS + 2 * STEPS
    rows = fields.shape[1] + 8 + 2 * PAD
    return pl.pallas_call(
        dynamics_kernel,
        out_shape=jax.ShapeDtypeStruct(fields.shape, F32),
        in_specs=[VM] * 6,
        out_specs=VM,
        scratch_shapes=[
            pltpu.VMEM((total, 2, rows, COLS), F32),
            pltpu.VMEM((total, 2, rows, COLS), F32),
            pltpu.VMEM((total, 8, COLS), jnp.int32),
            pltpu.VMEM((total, 8, COLS), F32),
        ],
        name="dynamics",
    )(fields, other, near, spread, left, right)


def silu(v):
    return (0.5 * v) * (1.0 + jnp.tanh(0.5 * v))


def networks_kernel(layers, inputs, outputs, chunk, *refs):
    parts, (same, cross, held, result, sems) = refs[:8], refs[8:]
    tile = lax.axis_index("tile")
    lev = lax.axis_index("lev")
    parity = tile % 2
    half = parts[2].shape[0]
    mine = pl.ds(pl.multiple_of(lev * half, 16), half)
    theirs = pl.ds(pl.multiple_of((1 - lev) * half, 16), half)
    where = [
        (0, parity, mine),
        (0, parity, theirs),
        (0, 1 - parity, mine),
        (0, 1 - parity, theirs),
        (1, parity, mine),
        (1, parity, theirs),
        (1, 1 - parity, mine),
        (1, 1 - parity, theirs),
    ]
    copies = []
    for i, (net, side, rows) in enumerate(where):
        source = parts[i].at[rows] if i < 2 else parts[i]
        copies.append(
            pltpu.make_async_copy(source, held.at[net, side, rows], sems.at[i])
        )
        copies[-1].start()
    depth = 2 * held.shape[3]
    tail = inputs + layers * depth
    bias = tail + outputs
    for net in range(2):
        for c in copies[4 * net : 4 * net + 4]:
            c.wait()
        x = jnp.concatenate([chunk[2 * net], chunk[2 * net + 1]], axis=1)
        hidden = None
        for layer in range(1 + layers):
            parts_out = []
            for side in range(2):
                shift = held[net, side, bias + layer : bias + layer + 1].astype(F32)
                if layer == 0:
                    dots = lax.dot_general(
                        x, held[net, side, 0:inputs], (((0,), (0,)), ((), ())),
                        preferred_element_type=F32,
                    )
                else:
                    top = inputs + (layer - 1) * depth
                    dots = jnp.dot(
                        hidden, held[net, side, top : top + depth],
                        preferred_element_type=F32,
                    )
                parts_out.append(silu(dots + shift).astype(BF16))
            hidden = jnp.concatenate(parts_out, axis=1)
        total = jnp.zeros((2 * COLS, outputs), F32)
        shift = jnp.zeros((1, outputs), F32)
        width = held.shape[3]
        for side in range(2):
            total = total + lax.dot_general(
                hidden[:, side * width : (side + 1) * width],
                held[net, side, tail:bias],
                (((1,), (1,)), ((), ())),
                preferred_element_type=F32,
            )
            row = bias + 1 + layers
            shift = shift + held[net, side, row : row + 1].astype(F32)[:, :outputs]
        done = (total + shift).T.astype(BF16)
        for i in range(2):
            result[2 * net + i] = done[:, i * COLS : (i + 1) * COLS]
    quarter = outputs // 4
    for i in range(4):
        for f in range(2):
            at = pl.multiple_of(2 * quarter * f + quarter * lev, quarter)
            off = pl.multiple_of(2 * quarter * f + quarter * (1 - lev), quarter)
            same[i, f * quarter : (f + 1) * quarter] = result[i, pl.ds(at, quarter)]
            cross[i, f * quarter : (f + 1) * quarter] = result[i, pl.ds(off, quarter)]


def networks(layers, inputs, outputs, chunk, parts):
    rows, width = parts[0].shape
    ends = jax.ShapeDtypeStruct((4, outputs // 2, COLS), BF16)
    return pl.pallas_call(
        functools.partial(networks_kernel, layers, inputs, outputs),
        out_shape=(ends, ends),
        in_specs=[VM] + [ANY] * 8,
        out_specs=(VM, VM),
        scratch_shapes=[
            pltpu.VMEM((2, 2, rows, width), BF16),
            pltpu.VMEM((4, outputs, COLS), BF16),
            pltpu.SemaphoreType.DMA((8,)),
        ],
        name="networks",
    )(chunk, *parts)


def combine_kernel(listed, owners, dynamics_in, *refs):
    positions = lax.axis_size("tile") // 4
    same, cross = refs[:positions], refs[positions : 2 * positions]
    out, table, seen = refs[2 * positions :]
    lev = lax.axis_index("lev")
    fill_slots(listed, owners, lev, table, 0, seen, -1)
    fill_slots(listed, owners, 1 - lev, table, 1, seen, -1)
    out[...] = dynamics_in[...]
    deep = out.shape[1]
    for row, group in ((0, same), (1, cross)):
        for m in range(positions):

            def add(i, carry, row=row, m=m, ref=group[m]):
                b = table[row, 4 * m + i]

                @pl.when(b >= 0)
                def _():
                    cols = block(b)
                    for f in range(2):
                        out[f, :, cols] += ref[i, f * deep : (f + 1) * deep].astype(F32)

                return carry

            lax.fori_loop(0, 4, add, 0)


def combined(listed, owners, dynamics_in, same, cross):
    positions = lax.axis_size("tile") // 4
    return pl.pallas_call(
        combine_kernel,
        out_shape=jax.ShapeDtypeStruct(dynamics_in.shape, F32),
        in_specs=[SM, SM] + [VM] * (1 + 2 * positions),
        out_specs=VM,
        scratch_shapes=[
            pltpu.SMEM((2, 4 * positions), jnp.int32),
            pltpu.SMEM((2 * positions,), jnp.int32),
        ],
        name="combine",
    )(listed, owners, dynamics_in, *same, *cross)


def local(
    fields,
    neighbors,
    diffusion,
    ancillary,
    listed,
    owners,
    first_weight,
    first_bias,
    middle_weight,
    middle_bias,
    last_weight,
    last_bias,
):
    tiles = lax.axis_size("tile")
    positions = tiles // 4
    state = 4 * fields.shape[1]
    layers = middle_weight.shape[1]
    outputs = last_weight.shape[2]
    flip = lambda mask: [(i, i ^ mask) for i in range(tiles)]
    swap = [(0, 1), (1, 0)]
    both = lambda mask: [
        (2 * i + l, 2 * (i ^ mask) + 1 - l) for i in range(tiles) for l in range(2)
    ]

    other = lax.ppermute(fields, "lev", swap)
    weights, part = joined_weights(
        state,
        first_weight[0],
        first_bias,
        middle_weight[0],
        middle_bias[0],
        last_weight[0],
        last_bias,
    )
    far = lax.ppermute(part, "tile", flip(tiles // 2))
    pair = lax.ppermute(part, "tile", flip(1))
    far_pair = lax.ppermute(far, "tile", flip(1))
    *chunks, to_next, to_last = dispatched(
        listed, owners, fields, other, neighbors, diffusion, ancillary
    )
    arrived = [chunks[0]] + [
        lax.ppermute(chunks[m], "tile", flip(2 * m)) for m in range(1, positions)
    ]
    left = lax.ppermute(to_next, "tile", [(i, (i + 1) % tiles) for i in range(tiles)])
    right = lax.ppermute(to_last, "tile", [((i + 1) % tiles, i) for i in range(tiles)])
    moved = dynamics(fields, other, neighbors, diffusion, left, right)
    pair_rest = lax.ppermute(pair, "lev", swap)
    far_rest = lax.ppermute(far, "lev", swap)
    far_pair_rest = lax.ppermute(far_pair, "lev", swap)
    parts = (weights, weights, pair, pair_rest, far, far_rest, far_pair, far_pair_rest)
    inputs = ceil16(first_weight.shape[1])
    same, cross = [], []
    for m in range(positions):
        near_rows, far_rows = networks(layers, inputs, outputs, arrived[m], parts)
        if m:
            near_rows = lax.ppermute(near_rows, "tile", flip(2 * m))
            far_rows = lax.ppermute(far_rows, ("tile", "lev"), both(2 * m))
        else:
            far_rows = lax.ppermute(far_rows, "lev", swap)
        same.append(near_rows)
        cross.append(far_rows)
    return combined(listed, owners, moved, same, cross)


def solution(mesh):
    return jax.shard_map(
        local,
        mesh=mesh,
        in_specs=(
            P(None, "lev", "tile"),
            P(None, "tile"),
            P(None, "tile"),
            P(None, "tile"),
            P("tile", None),
            P("tile", None),
            P("tile", None, None),
            P("tile", None),
            P("tile", None, None, None),
            P("tile", None, None),
            P("tile", None, None),
            P("tile", None),
        ),
        out_specs=P(None, "lev", "tile"),
        check_vma=False,
    )
```
